128 devices in a mesh: row: 8 (over z, core), col: 4 (over y), depth: 4 (over x).
Axes of the slice: x: 4, y: 4, z: 4, core: 2. Of those that a mesh axis runs over, the one named last changes fastest.
Arguments:
- traces: bfloat16 [32768, 16384], P(('col', 'depth'), 'row'), may hold values from -0.03125 to 0.03125
- features: bfloat16 [32768, 2048], P(('col', 'depth'), 'row'), may hold values from -6 to 6
- next_features: bfloat16 [32768, 2048], P(('col', 'depth'), 'row'), may hold values from -6 to 6
Outputs:
- panels: float32 [16384, 2048], P('row', ('col', 'depth'))
The draws below stay inside these ranges and needn't reach their ends.
All inputs are finite; a program needn't handle non-finite values.
Results may differ from the reference program's by a relative error of at most 0.0028.
Values may be sent and summed in bfloat16 or wider, within the bound.
A program may use at most 128 MiB of HBM per device.

```python
import jax
import jax.numpy as jnp
from jax import lax

F = 16384
PW = 1024
PANELS = 2
TOKENS = 32768


def spiked(entries, key, source, target, parts, factor):
    owner, partner = [(jnp.arange(entries.shape[position]) // (entries.shape[position] // parts)).reshape([-1 if axis == position else 1 for axis in range(entries.ndim)]) for position in (source, target)]
    chosen = jax.random.permutation(key, parts)[partner]
    strong = (owner == chosen) | (owner == (partner + parts // 2) % parts)
    return jnp.where(strong, factor * entries, entries)


def block_levels(key, shape, pieces, least, largest):
    level = 1.0
    for position, shards_of in pieces:
        heights = jax.random.uniform(jax.random.fold_in(jax.random.fold_in(key, 6), position), (shards_of,), jnp.float32, least / len(pieces), largest / len(pieces))
        level = level * jnp.repeat(jnp.exp(heights), shape[position] // shards_of).reshape((-1,) + (1,) * (len(shape) - 1 - position))
    return level


def normal_values(own_key, dims, spread, most, shards=(), held_as=jnp.bfloat16):
    array = jax.random.normal(own_key, dims, jnp.float32) * spread
    if len(shards) > 0:
        array = block_levels(own_key, dims, shards, -0.22, 0.18) * array
    return jnp.clip(array, min=-most, max=most).astype(held_as)


def heavy_noise(key, shape, scale, reach, pieces, heavy, held_as=jnp.bfloat16):
    result = scale * jax.random.normal(key, shape, jnp.float32)
    if pieces:
        result = result * block_levels(key, shape, pieces, -0.22, 0.18)
    return jnp.clip(spiked(result, jax.random.fold_in(key, 3), *heavy), -reach, reach).astype(held_as)


def setup_inputs(seed: int = 0) -> dict:
    seeds = jax.random.split(jax.random.key(seed), 4)
    return {
        "traces": normal_values(seeds[0], (TOKENS, F), TOKENS ** -0.5, 0.03125, ((0, 16), (1, 8))),
        "features": heavy_noise(seeds[1], (TOKENS, PANELS * PW), 1.0, 6.0, ((0, 16), (1, 8)), (0, 1, 16, 2.0)),
        "next_features": normal_values(seeds[2], (TOKENS, PANELS * PW), 1.0, 6.0, ((0, 16), (1, 8))),
    }


DISCOUNT = 0.99


def reference(traces, features, next_features):
    differences = (features.astype(jnp.float32) - DISCOUNT * next_features.astype(jnp.float32)).astype(jnp.bfloat16)
    differences = lax.optimization_barrier(differences).astype(jnp.float32)
    weights = traces.astype(jnp.float32)
    return lax.dot_general(weights, differences, (((0,), (0,)), ((), ())), precision=lax.Precision.HIGHEST, preferred_element_type=jnp.float32)
```

```python
import jax
import jax.numpy as jnp
from jax import lax
from jax.experimental import pallas as pl
from jax.experimental.pallas import tpu as pltpu
from jax.sharding import PartitionSpec as P

DISCOUNT = 0.99
MESH = pl.DeviceIdType.MESH
F32, BF16 = jnp.float32, jnp.bfloat16
TILE = 256
UNIT = 16

UNITS = [2, 2, 2, 2]
AHEAD = 2
BATCHES = [
    [(0, 0), (0, 1)],
    [(0, 2), (0, 3)],
    [(1, 0), (3, 0)],
    [(1, 1), (3, 1)],
    [(2, 0), (2, 1)],
    [(1, 2), (3, 2)],
    [(1, 3), (3, 3)],
    [(2, 2), (2, 3)],
]
SPLIT = [1536, 1280, 1280, 1024, 1536, 768, 1024, 1536]
SCHEDULE = [
    "c0", "y10", "x10", "c1", "f0", "x11", "x20", "y20", "f1", "c2", "y12", "x12", "c3", "x13", "r0", "y22",
    "y13", "y30", "f2", "x21", "x23", "y23", "y32", "x22", "r1", "y11", "c5", "x15", "y15", "c4", "x14", "f3",
    "x31", "x32", "x33", "y14", "x30", "y40", "x25", "c6", "y16", "r2", "r3", "x24", "y25", "y21", "y24", "x16",
    "c7", "y17", "x17", "x26", "x34", "x41", "y33", "y50", "y34", "x40", "y27", "y26", "x27", "x44", "y44", "y35",
    "x36", "x35", "x51", "y43", "y31", "x37", "x42", "y36", "y45", "y41", "y37", "x47", "y46", "y42", "x43", "x54",
    "x46", "y54", "y55", "x45", "x53", "y47", "y57", "y53", "y56", "x56", "x55", "x57", "x50", "x52", "y51", "y52",
]

PIECES = len(UNITS)
FIRST = [sum(UNITS[:k]) for k in range(PIECES + 1)]
BASE = {}
for _groups in BATCHES:
    for _s, _k in _groups:
        BASE[_s, _k] = sum(4 * UNITS[k] for s, k in BASE)
CHUNK = {g: BASE[g] // 4 for g in BASE}
INDEX = {g: i for i, g in enumerate(BASE)}
ALL = FIRST[-1]
WX, WY = max(SPLIT), 2048 - min(SPLIT)


def kernel(
    traces, features, nexts, out,
    feat, nxt, weights, diff, p, pf, total,
    xda, xdb, xl, xr, xa, zd, za, zl, zr, wd, wa, wl, wr, vda, vdb, vl, vr, va,
    load, load_t, part, ring, ring_a, ring_b, ag_send,
    s_xda, s_xdb, s_xl, s_xr, s_x, s_zd, s_zl, s_zr, s_z, s_wd, s_wl, s_wr, s_w,
    s_vda, s_vdb, s_vl, s_vr, s_v,
):
    r, y, x = lax.axis_index("row"), lax.axis_index("col"), lax.axis_index("depth")
    z, h = r // 2, r % 2
    xp, xm, x2 = (x + 1) % 4, (x + 3) % 4, (x + 2) % 4
    east, west = {"depth": xp}, {"depth": xm}
    north, south = {"col": (y + 1) % 4}, {"col": (y + 3) % 4}
    up, down = {"row": (z + 1) % 4 * 2 + h}, {"row": (z + 3) % 4 * 2 + h}
    partner = {"row": z * 2 + 1 - h}
    tiles, rows = weights.shape[0], total.shape[-1]

    def send(src, dst, send_sem, recv_sem, where):
        pltpu.make_async_remote_copy(
            src_ref=src, dst_ref=dst, send_sem=send_sem, recv_sem=recv_sem, device_id=where, device_id_type=MESH
        ).start()

    def wait(ref, sem):
        pltpu.make_async_copy(ref, ref, sem).wait()

    first = [pltpu.make_async_copy(features, feat, load.at[0]), pltpu.make_async_copy(nexts, nxt, load.at[1])]
    for copy in first:
        copy.start()
    barrier = pltpu.get_barrier_semaphore()
    for where in (east, west, north, south, up, down, partner):
        pl.semaphore_signal(barrier, inc=1, device_id=where, device_id_type=MESH)

    def weight(t):
        columns = pl.ds(pl.multiple_of(t * TILE, TILE), TILE)
        return pltpu.make_async_copy(traces.at[:, columns], weights.at[t], load_t.at[t])

    for copy in first:
        copy.wait()
    for t in range(tiles):
        weight(t).start()

    @pl.loop(0, feat.shape[0] // 128)
    def _(t):
        tokens = pl.ds(pl.multiple_of(t * 128, 128), 128)
        d = feat[tokens, :].astype(F32) - DISCOUNT * nxt[tokens, :].astype(F32)
        d = d.astype(BF16).T.reshape(2, ALL, UNIT, 128)
        for b in range(2):
            for k in range(PIECES):
                u = UNITS[k]
                diff[pl.ds(BASE[0, k] + (2 * h + b) * u, u), :, tokens] = d[b, FIRST[k] : FIRST[k] + u]

    pl.semaphore_wait(barrier, 7)


    def mine(g):
        u = UNITS[g[1]]
        return diff.at[pl.ds(BASE[g] + 2 * h * u, 2 * u)]

    def theirs(g):
        u = UNITS[g[1]]
        return diff.at[pl.ds(BASE[g] + 2 * (1 - h) * u, 2 * u)]

    def one(g, b):
        u = UNITS[g[1]]
        return diff.at[pl.ds(BASE[g] + (2 * h + b) * u, u)]

    def ring_out(k):
        if k >= PIECES:
            return
        send(mine((0, k)), mine((3, k)), ag_send.at[INDEX[0, k]], ring.at[INDEX[3, k]], up)
        send(mine((0, k)), mine((1, k)), ag_send.at[INDEX[0, k]], ring.at[INDEX[1, k]], down)

    def to_partner(g):
        send(mine(g), mine(g), ag_send.at[INDEX[g]], part.at[INDEX[g]], partner)

    def forward(k):
        below, above, far = (3, k), (1, k), (2, k)
        wait(mine(below), ring.at[INDEX[below]])
        send(one(below, 0), one(far, 0), ag_send.at[INDEX[below]], ring_a.at[k], up)
        wait(mine(above), ring.at[INDEX[above]])
        send(one(above, 1), one(far, 1), ag_send.at[INDEX[above]], ring_b.at[k], down)
        ring_out(k + AHEAD)
        to_partner(below)
        to_partner(above)

    def far_end(k):
        far = (2, k)
        wait(one(far, 0), ring_a.at[k])
        wait(one(far, 1), ring_b.at[k])
        to_partner(far)


    def chunk(ref, g, i, lo, hi):
        u = UNITS[g[1]]
        return ref.at[pl.ds(BASE[g] + i * u, u), :, lo:hi]

    def exchange(g, lo, mid, hi, at, j, da, db, left, right, sends, s_da, s_db, s_l, s_r):
        n = mid - lo
        send(chunk(p, g, x2, lo, mid), da.at[at, :, 0:n], sends.at[j], s_da.at[j], east)
        send(chunk(p, g, x2, mid, hi), db.at[at, :, 0:n], sends.at[j], s_db.at[j], west)
        send(chunk(p, g, xp, mid, hi), left.at[at, :, n : 2 * n], sends.at[j], s_l.at[j], east)
        send(chunk(p, g, xm, lo, mid), right.at[at, :, 0:n], sends.at[j], s_r.at[j], west)

    def pass_on(g, lo, mid, hi, at, j, da, db, left, right, acc, sends, s_da, s_db, s_l, s_r):
        n = mid - lo
        wait(da.at[at, :, 0:n], s_da.at[j])
        acc[at, :, 0:n] = (chunk(pf, g, xp, lo, mid)[...] + da[at, :, 0:n].astype(F32)).astype(BF16)
        send(acc.at[at, :, 0:n], left.at[at, :, 0:n], sends.at[j], s_l.at[j], east)
        wait(db.at[at, :, 0:n], s_db.at[j])
        acc[at, :, n : 2 * n] = (chunk(pf, g, xm, mid, hi)[...] + db[at, :, 0:n].astype(F32)).astype(BF16)
        send(acc.at[at, :, n : 2 * n], right.at[at, :, n : 2 * n], sends.at[j], s_r.at[j], west)

    def parts(g):
        u = UNITS[g[1]]
        return pl.ds(CHUNK[g], u), INDEX[g], pl.ds(FIRST[g[1]], u), g[1]

    def x1(g, w, dy):
        at, j, _, _ = parts(g)
        exchange(g, 0, w // 2, w, at, j, xda, xdb, xl, xr, s_x, s_xda, s_xdb, s_xl, s_xr)

    def x2_(g, w, dy):
        at, j, _, _ = parts(g)
        pass_on(g, 0, w // 2, w, at, j, xda, xdb, xl, xr, xa, s_x, s_xda, s_xdb, s_xl, s_xr)

    def x3(g, w, dy):
        at, j, to, k = parts(g)
        n = w // 2
        wait(xl.at[at, :, 0:w], s_xl.at[j])
        wait(xr.at[at, :, 0:w], s_xr.at[j])
        own = chunk(pf, g, x, 0, w)
        summed = own[...] + xl[at, :, 0:w].astype(F32) + xr[at, :, 0:w].astype(F32)

        @pl.when(dy == 0)
        def _():
            total[to, :, 0:w] = summed

        @pl.when(dy != 0)
        def _():
            own[...] = summed
            chunk(p, g, x, 0, w)[...] = summed.astype(BF16)

        a, b = chunk(p, g, x, 0, n), chunk(p, g, x, n, w)

        @pl.when(dy == 2)
        def _():
            send(a, zd.at[at, :, 0:n], s_z.at[j], s_zd.at[j], south)
            send(b, zd.at[at, :, 0:n], s_z.at[j], s_zd.at[j], north)

        @pl.when(dy == 1)
        def _():
            send(b, zr.at[to, :, n:w], s_z.at[j], s_zr.at[k], south)

        @pl.when(dy == 3)
        def _():
            send(a, zl.at[to, :, 0:n], s_z.at[j], s_zl.at[k], north)

    def x4(g, w, dy):
        at, j, to, k = parts(g)
        n = w // 2

        @pl.when(dy == 1)
        def _():
            wait(zd.at[at, :, 0:n], s_zd.at[j])
            za[at, :, 0:n] = (chunk(pf, g, x, 0, n)[...] + zd[at, :, 0:n].astype(F32)).astype(BF16)
            send(za.at[at, :, 0:n], zr.at[to, :, 0:n], s_z.at[j], s_zr.at[k], south)

        @pl.when(dy == 3)
        def _():
            wait(zd.at[at, :, 0:n], s_zd.at[j])
            za[at, :, 0:n] = (chunk(pf, g, x, n, w)[...] + zd[at, :, 0:n].astype(F32)).astype(BF16)
            send(za.at[at, :, 0:n], zl.at[to, :, n:w], s_z.at[j], s_zl.at[k], north)

    def x5(g, w, dy):
        _, _, to, k = parts(g)

        @pl.when(dy == 0)
        def _():
            wait(zl.at[to, :, 0:w], s_zl.at[k])
            wait(zr.at[to, :, 0:w], s_zr.at[k])
            total[to, :, 0:w] += zl[to, :, 0:w].astype(F32) + zr[to, :, 0:w].astype(F32)

    def wide(g):
        u = UNITS[g[1]]
        return pl.ds(2 * CHUNK[g], 2 * u), 4 * FIRST[g[1]], 2 * u, BASE[g]

    def y1(g, w, dy):
        at, to, u, base = wide(g)
        _, j, _, k = parts(g)
        n = rows - w
        a, b = p.at[base : base + u, :, w:rows], p.at[base + u : base + 2 * u, :, w:rows]

        @pl.when(dy == 2)
        def _():
            send(a, wd.at[at, :, 0:n], s_w.at[j], s_wd.at[j], south)
            send(b, wd.at[at, :, 0:n], s_w.at[j], s_wd.at[j], north)

        @pl.when(dy == 1)
        def _():
            send(b, wr.at[to + u : to + 2 * u, :, 0:n], s_w.at[j], s_wr.at[k], south)

        @pl.when(dy == 3)
        def _():
            send(a, wl.at[to : to + u, :, 0:n], s_w.at[j], s_wl.at[k], north)

    def y2(g, w, dy):
        at, to, u, base = wide(g)
        _, j, _, k = parts(g)
        n = rows - w

        @pl.when(dy == 1)
        def _():
            wait(wd.at[at, :, 0:n], s_wd.at[j])
            wa[at, :, 0:n] = (pf[base : base + u, :, w:rows] + wd[at, :, 0:n].astype(F32)).astype(BF16)
            send(wa.at[at, :, 0:n], wr.at[to : to + u, :, 0:n], s_w.at[j], s_wr.at[k], south)

        @pl.when(dy == 3)
        def _():
            wait(wd.at[at, :, 0:n], s_wd.at[j])
            wa[at, :, 0:n] = (pf[base + u : base + 2 * u, :, w:rows] + wd[at, :, 0:n].astype(F32)).astype(BF16)
            send(wa.at[at, :, 0:n], wl.at[to + u : to + 2 * u, :, 0:n], s_w.at[j], s_wl.at[k], north)

    def y3(g, w, dy):
        _, to, u, base = wide(g)
        at, j, to1, k = parts(g)
        n = rows - w

        @pl.when(dy == 0)
        def _():
            wait(wl.at[to : to + 2 * u, :, 0:n], s_wl.at[k])
            wait(wr.at[to : to + 2 * u, :, 0:n], s_wr.at[k])

            @pl.loop(0, 2 * u)
            def _(i):
                summed = pf[base + i, :, w:rows] + wl[to + i, :, 0:n].astype(F32) + wr[to + i, :, 0:n].astype(F32)
                pf[base + i, :, w:rows] = summed
                p[base + i, :, w:rows] = summed.astype(BF16)

            exchange(g, w, (w + rows) // 2, rows, to1, k, vda, vdb, vl, vr, s_v, s_vda, s_vdb, s_vl, s_vr)

    def y4(g, w, dy):
        _, _, to, k = parts(g)

        @pl.when(dy == 0)
        def _():
            pass_on(g, w, (w + rows) // 2, rows, to, k, vda, vdb, vl, vr, va, s_v, s_vda, s_vdb, s_vl, s_vr)

    def y5(g, w, dy):
        _, _, to, k = parts(g)
        n = rows - w

        @pl.when(dy == 0)
        def _():
            wait(vl.at[to, :, 0:n], s_vl.at[k])
            wait(vr.at[to, :, 0:n], s_vr.at[k])
            total[to, :, w:rows] = (
                chunk(pf, g, x, w, rows)[...] + vl[to, :, 0:n].astype(F32) + vr[to, :, 0:n].astype(F32)
            )

    stages = {"x1": x1, "x2": x2_, "x3": x3, "x4": x4, "x5": x5, "y1": y1, "y2": y2, "y3": y3, "y4": y4, "y5": y5}
    loaded = []

    def compute(batch):
        groups = BATCHES[batch]
        for g in groups:
            wait(theirs(g), part.at[INDEX[g]])
        start, count = BASE[groups[0]], sum(4 * UNITS[k] for _, k in groups)
        unloaded = not loaded
        loaded.append(batch)

        @pl.loop(0, tiles)
        def _(t):
            if unloaded:
                weight(t).wait()
            left = diff[start : start + count].reshape(count * UNIT, diff.shape[-1])
            product = jnp.dot(left, weights[t], preferred_element_type=F32).reshape(count, UNIT, TILE)
            columns = pl.ds(pl.multiple_of(t * TILE, TILE), TILE)
            pf[start : start + count, :, columns] = product
            p[start : start + count, :, columns] = product.astype(BF16)

    for k in range(PIECES):
        to_partner((0, k))
        if k < AHEAD:
            ring_out(k)

    for step in SCHEDULE:
        name, n = step[:-1], int(step[-1])
        if name == "f":
            forward(n)
        elif name == "r":
            far_end(n)
        elif name == "c":
            compute(n)
        else:
            for g in BATCHES[n]:
                stages[name](g, SPLIT[n], (y - z - g[0] + 8) % 4)

    @pl.loop(0, rows // 128)
    def _(t):
        columns = pl.ds(pl.multiple_of(t * 128, 128), 128)
        out[columns, :] = total[:, :, columns].reshape(128, 128).T

    for batch, groups in enumerate(BATCHES):
        w = SPLIT[batch]
        for s, k in groups:
            j, u = INDEX[s, k], UNITS[k]
            wait(diff.at[0 : (6, 3, 2, 3)[s] * u], ag_send.at[j])
            wait(p.at[0 : 3 * u, :, 0:w], s_x.at[j])

            @pl.when((y - z - s + 8) % 4 != 0)
            def _():
                wait(p.at[0:u, :, 0:w], s_z.at[j])
                wait(p.at[0 : 4 * u, :, w:rows], s_w.at[j])

            @pl.when((y - z - s + 8) % 4 == 0)
            def _():
                wait(p.at[0 : 3 * u, :, w:rows], s_v.at[k])


def shards(traces, features, nexts):
    tokens, rows = traces.shape
    groups = len(BASE)
    vmem, dma = pltpu.VMEM, pltpu.SemaphoreType.DMA
    of_groups, of_pieces = dma((groups,)), dma((PIECES,))
    scratch = [
        vmem(features.shape, BF16), vmem(features.shape, BF16),
        vmem((rows // TILE, tokens, TILE), BF16),
        vmem((16 * ALL, UNIT, tokens), BF16),
        vmem((16 * ALL, UNIT, rows), BF16), vmem((16 * ALL, UNIT, rows), F32),
        vmem((ALL, UNIT, rows), F32),
        vmem((4 * ALL, UNIT, WX // 2), BF16), vmem((4 * ALL, UNIT, WX // 2), BF16),
        vmem((4 * ALL, UNIT, WX), BF16), vmem((4 * ALL, UNIT, WX), BF16), vmem((4 * ALL, UNIT, WX), BF16),
        vmem((4 * ALL, UNIT, WX // 2), BF16), vmem((4 * ALL, UNIT, WX // 2), BF16),
        vmem((ALL, UNIT, WX), BF16), vmem((ALL, UNIT, WX), BF16),
        vmem((8 * ALL, UNIT, WY), BF16), vmem((8 * ALL, UNIT, WY), BF16),
        vmem((4 * ALL, UNIT, WY), BF16), vmem((4 * ALL, UNIT, WY), BF16),
        vmem((ALL, UNIT, WY // 2), BF16), vmem((ALL, UNIT, WY // 2), BF16),
        vmem((ALL, UNIT, WY), BF16), vmem((ALL, UNIT, WY), BF16), vmem((ALL, UNIT, WY), BF16),
        dma((2,)), dma((rows // TILE,)), of_groups, of_groups, of_pieces, of_pieces, of_groups,
        of_groups, of_groups, of_groups, of_groups, of_groups,
        of_groups, of_pieces, of_pieces, of_groups,
        of_groups, of_pieces, of_pieces, of_groups,
        of_pieces, of_pieces, of_pieces, of_pieces, of_pieces,
    ]
    return pl.pallas_call(
        kernel,
        out_shape=jax.ShapeDtypeStruct((rows, features.shape[1] // 2), F32),
        in_specs=[pl.BlockSpec(memory_space=pl.ANY)] * 3,
        out_specs=pl.BlockSpec(memory_space=pltpu.VMEM),
        scratch_shapes=scratch,
        compiler_params=pltpu.CompilerParams(
            collective_id=0, has_side_effects=True, vmem_limit_bytes=67043328
        ),
        name="panels",
    )(traces, features, nexts)


def solution(mesh):
    return jax.shard_map(
        shards,
        mesh=mesh,
        in_specs=(P(("col", "depth"), "row"), P(("col", "depth"), "row"), P(("col", "depth"), "row")),
        out_specs=P("row", ("col", "depth")),
        check_vma=False,
    )
```

```python
import jax
import jax.numpy as jnp
from jax import lax
from jax.experimental import pallas as pl
from jax.experimental.pallas import tpu as pltpu
from jax.sharding import PartitionSpec as P

DISCOUNT = 0.99
MESH = pl.DeviceIdType.MESH
F32, BF16 = jnp.float32, jnp.bfloat16
TILE = 1024
CHUNKS = 4
UNIT = 16

UNITS = [2, 2, 2, 2]
AHEAD = 2
BATCHES = [
    [(0, 0), (0, 1)],
    [(0, 2), (0, 3)],
    [(1, 0), (3, 0)],
    [(1, 1), (3, 1)],
    [(2, 0)],
    [(1, 2), (3, 2)],
    [(2, 1)],
    [(1, 3), (3, 3)],
    [(2, 2)],
    [(2, 3)],
]
SPLIT = [1024, 1280, 1024, 1024, 1280, 1536, 1536, 1024, 1536, 1280]
SCHEDULE = [
    "c.0", "y1.0", "x1.0", "c.1", "y1.1", "x1.1", "f.0", "x2.0", "c.2", "y1.2", "f.1", "x2.1", "x1.2", "c.3",
    "y1.3", "x1.3", "r.0", "c.4", "x1.4", "y1.4", "x2.2", "f.2", "y2.1", "x2.3", "y2.2", "x2.4", "c.5", "y1.5",
    "x1.5", "r.1", "y2.4", "x3.3", "x3.4", "c.6", "x1.6", "y1.6", "f.3", "x3.0", "y2.3", "x2.5", "x3.2", "y2.6",
    "c.7", "y1.7", "x1.7", "x4.0", "x4.3", "r.2", "x2.6", "r.3", "x3.1", "x4.4", "c.8", "x1.8", "y1.8", "c.9",
    "y1.9", "y3.4", "y2.0", "y3.1", "x5.0", "y2.7", "y3.6", "y2.5", "x1.9", "y2.8", "x2.7", "x3.5", "y3.8", "x4.2",
    "x5.4", "y2.9", "x4.1", "x3.6", "x2.8", "x2.9", "y3.0", "y3.2", "y3.3", "y3.9", "x3.8", "y4.4", "x3.9", "y3.5",
    "x4.5", "x3.7", "y4.1", "y4.6", "y3.7", "x5.2", "y4.0", "y4.9", "y4.2", "x5.1", "y5.4", "x4.6", "y4.3", "y4.8",
    "x5.3", "x4.7", "y5.8", "x4.8", "x5.6", "y5.1", "y5.0", "y4.7", "y5.9", "x5.8", "x4.9", "y4.5", "y5.3", "x5.5",
    "y5.2", "y5.7", "x5.7", "y5.6", "y5.5", "x5.9",
]

PIECES = len(UNITS)
FIRST = [sum(UNITS[:k]) for k in range(PIECES + 1)]
BASE = {}
for _groups in BATCHES:
    for _s, _k in _groups:
        BASE[_s, _k] = sum(4 * UNITS[k] for s, k in BASE)
CHUNK = {g: BASE[g] // 4 for g in BASE}
INDEX = {g: i for i, g in enumerate(BASE)}
ALL = FIRST[-1]
WX, WY = max(SPLIT), 2048 - min(SPLIT)


def kernel(
    traces, features, nexts, total,
    feat, nxt, weights, diff, p, pf,
    xda, xdb, xl, xr, xa, zd, za, zl, zr, wd, wa, wl, wr, vda, vdb, vl, vr, va,
    load, load_t, part, ring, ring_a, ring_b, ag_send,
    s_xda, s_xdb, s_xl, s_xr, s_x, s_zd, s_zl, s_zr, s_z, s_wd, s_wl, s_wr, s_w,
    s_vda, s_vdb, s_vl, s_vr, s_v,
):
    r, y, x = lax.axis_index("row"), lax.axis_index("col"), lax.axis_index("depth")
    z, h = r // 2, r % 2
    xp, xm, x2 = (x + 1) % 4, (x + 3) % 4, (x + 2) % 4
    east, west = {"depth": xp}, {"depth": xm}
    north, south = {"col": (y + 1) % 4}, {"col": (y + 3) % 4}
    up, down = {"row": (z + 1) % 4 * 2 + h}, {"row": (z + 3) % 4 * 2 + h}
    partner = {"row": z * 2 + 1 - h}
    tiles, rows = weights.shape[0], total.shape[-1]

    def send(src, dst, send_sem, recv_sem, where):
        pltpu.make_async_remote_copy(
            src_ref=src, dst_ref=dst, send_sem=send_sem, recv_sem=recv_sem, device_id=where, device_id_type=MESH
        ).start()

    def wait(ref, sem):
        pltpu.make_async_copy(ref, ref, sem).wait()

    tokens = feat.shape[0] // CHUNKS

    def loads(c):
        some = pl.ds(c * tokens, tokens)
        return [
            pltpu.make_async_copy(features.at[some], feat.at[some], load.at[c]),
            pltpu.make_async_copy(nexts.at[some], nxt.at[some], load.at[CHUNKS + c]),
        ]

    for c in range(CHUNKS):
        for copy in loads(c):
            copy.start()
    barrier = pltpu.get_barrier_semaphore()
    for where in (east, west, north, south, up, down, partner):
        pl.semaphore_signal(barrier, inc=1, device_id=where, device_id_type=MESH)

    def weight(t):
        columns = pl.ds(pl.multiple_of(t * TILE, TILE), TILE)
        return pltpu.make_async_copy(traces.at[:, columns], weights.at[t], load_t.at[t])

    for c in range(CHUNKS):
        for copy in loads(c):
            copy.wait()
        if c == CHUNKS - 1:
            for t in range(tiles):
                weight(t).start()

        @pl.loop(c * tokens // 128, (c + 1) * tokens // 128)
        def _(t):
            some = pl.ds(pl.multiple_of(t * 128, 128), 128)
            d = feat[some, :].astype(F32) - DISCOUNT * nxt[some, :].astype(F32)
            d = d.astype(BF16).T.reshape(2, ALL, UNIT, 128)
            for b in range(2):
                for k in range(PIECES):
                    u = UNITS[k]
                    diff[pl.ds(BASE[0, k] + (2 * h + b) * u, u), :, some] = d[b, FIRST[k] : FIRST[k] + u]

    pl.semaphore_wait(barrier, 7)


    def mine(g):
        u = UNITS[g[1]]
        return diff.at[pl.ds(BASE[g] + 2 * h * u, 2 * u)]

    def theirs(g):
        u = UNITS[g[1]]
        return diff.at[pl.ds(BASE[g] + 2 * (1 - h) * u, 2 * u)]

    def one(g, b):
        u = UNITS[g[1]]
        return diff.at[pl.ds(BASE[g] + (2 * h + b) * u, u)]

    def ring_out(k):
        if k >= PIECES:
            return
        send(mine((0, k)), mine((3, k)), ag_send.at[INDEX[0, k]], ring.at[INDEX[3, k]], up)
        send(mine((0, k)), mine((1, k)), ag_send.at[INDEX[0, k]], ring.at[INDEX[1, k]], down)

    def to_partner(g):
        send(mine(g), mine(g), ag_send.at[INDEX[g]], part.at[INDEX[g]], partner)

    def forward(k):
        below, above, far = (3, k), (1, k), (2, k)
        wait(mine(below), ring.at[INDEX[below]])
        send(one(below, 0), one(far, 0), ag_send.at[INDEX[below]], ring_a.at[k], up)
        wait(mine(above), ring.at[INDEX[above]])
        send(one(above, 1), one(far, 1), ag_send.at[INDEX[above]], ring_b.at[k], down)
        ring_out(k + AHEAD)
        to_partner(below)
        to_partner(above)

    def far_end(k):
        far = (2, k)
        wait(one(far, 0), ring_a.at[k])
        wait(one(far, 1), ring_b.at[k])
        to_partner(far)


    def chunk(ref, g, i, lo, hi):
        u = UNITS[g[1]]
        return ref.at[pl.ds(BASE[g] + i * u, u), :, lo:hi]

    def exchange(g, lo, mid, hi, at, j, da, db, left, right, sends, s_da, s_db, s_l, s_r):
        n = mid - lo
        send(chunk(p, g, x2, lo, mid), da.at[at, :, 0:n], sends.at[j], s_da.at[j], east)
        send(chunk(p, g, x2, mid, hi), db.at[at, :, 0:n], sends.at[j], s_db.at[j], west)
        send(chunk(p, g, xp, mid, hi), left.at[at, :, n : 2 * n], sends.at[j], s_l.at[j], east)
        send(chunk(p, g, xm, lo, mid), right.at[at, :, 0:n], sends.at[j], s_r.at[j], west)

    def pass_on(g, lo, mid, hi, at, j, da, db, left, right, acc, sends, s_da, s_db, s_l, s_r):
        n = mid - lo
        wait(da.at[at, :, 0:n], s_da.at[j])
        acc[at, :, 0:n] = (chunk(pf, g, xp, lo, mid)[...] + da[at, :, 0:n].astype(F32)).astype(BF16)
        send(acc.at[at, :, 0:n], left.at[at, :, 0:n], sends.at[j], s_l.at[j], east)
        wait(db.at[at, :, 0:n], s_db.at[j])
        acc[at, :, n : 2 * n] = (chunk(pf, g, xm, mid, hi)[...] + db[at, :, 0:n].astype(F32)).astype(BF16)
        send(acc.at[at, :, n : 2 * n], right.at[at, :, n : 2 * n], sends.at[j], s_r.at[j], west)

    def parts(g):
        u = UNITS[g[1]]
        return pl.ds(CHUNK[g], u), INDEX[g], pl.ds(FIRST[g[1]], u), g[1]

    def x1(g, w, dy):
        at, j, _, _ = parts(g)
        exchange(g, 0, w // 2, w, at, j, xda, xdb, xl, xr, s_x, s_xda, s_xdb, s_xl, s_xr)

    def x2_(g, w, dy):
        at, j, _, _ = parts(g)
        pass_on(g, 0, w // 2, w, at, j, xda, xdb, xl, xr, xa, s_x, s_xda, s_xdb, s_xl, s_xr)

    def x3(g, w, dy):
        at, j, to, k = parts(g)
        n = w // 2
        wait(xl.at[at, :, 0:w], s_xl.at[j])
        wait(xr.at[at, :, 0:w], s_xr.at[j])
        own = chunk(pf, g, x, 0, w)
        summed = own[...] + xl[at, :, 0:w].astype(F32) + xr[at, :, 0:w].astype(F32)

        @pl.when(dy == 0)
        def _():
            total[to, :, 0:w] = summed

        @pl.when(dy != 0)
        def _():
            own[...] = summed
            chunk(p, g, x, 0, w)[...] = summed.astype(BF16)

        a, b = chunk(p, g, x, 0, n), chunk(p, g, x, n, w)

        @pl.when(dy == 2)
        def _():
            send(a, zd.at[at, :, 0:n], s_z.at[j], s_zd.at[j], south)
            send(b, zd.at[at, :, 0:n], s_z.at[j], s_zd.at[j], north)

        @pl.when(dy == 1)
        def _():
            send(b, zr.at[to, :, n:w], s_z.at[j], s_zr.at[k], south)

        @pl.when(dy == 3)
        def _():
            send(a, zl.at[to, :, 0:n], s_z.at[j], s_zl.at[k], north)

    def x4(g, w, dy):
        at, j, to, k = parts(g)
        n = w // 2

        @pl.when(dy == 1)
        def _():
            wait(zd.at[at, :, 0:n], s_zd.at[j])
            za[at, :, 0:n] = (chunk(pf, g, x, 0, n)[...] + zd[at, :, 0:n].astype(F32)).astype(BF16)
            send(za.at[at, :, 0:n], zr.at[to, :, 0:n], s_z.at[j], s_zr.at[k], south)

        @pl.when(dy == 3)
        def _():
            wait(zd.at[at, :, 0:n], s_zd.at[j])
            za[at, :, 0:n] = (chunk(pf, g, x, n, w)[...] + zd[at, :, 0:n].astype(F32)).astype(BF16)
            send(za.at[at, :, 0:n], zl.at[to, :, n:w], s_z.at[j], s_zl.at[k], north)

    def x5(g, w, dy):
        _, _, to, k = parts(g)

        @pl.when(dy == 0)
        def _():
            wait(zl.at[to, :, 0:w], s_zl.at[k])
            wait(zr.at[to, :, 0:w], s_zr.at[k])
            total[to, :, 0:w] += zl[to, :, 0:w].astype(F32) + zr[to, :, 0:w].astype(F32)

    def wide(g):
        u = UNITS[g[1]]
        return pl.ds(2 * CHUNK[g], 2 * u), 4 * FIRST[g[1]], 2 * u, BASE[g]

    def y1(g, w, dy):
        at, to, u, base = wide(g)
        _, j, _, k = parts(g)
        n = rows - w
        a, b = p.at[base : base + u, :, w:rows], p.at[base + u : base + 2 * u, :, w:rows]

        @pl.when(dy == 2)
        def _():
            send(a, wd.at[at, :, 0:n], s_w.at[j], s_wd.at[j], south)
            send(b, wd.at[at, :, 0:n], s_w.at[j], s_wd.at[j], north)

        @pl.when(dy == 1)
        def _():
            send(b, wr.at[to + u : to + 2 * u, :, 0:n], s_w.at[j], s_wr.at[k], south)

        @pl.when(dy == 3)
        def _():
            send(a, wl.at[to : to + u, :, 0:n], s_w.at[j], s_wl.at[k], north)

    def y2(g, w, dy):
        at, to, u, base = wide(g)
        _, j, _, k = parts(g)
        n = rows - w

        @pl.when(dy == 1)
        def _():
            wait(wd.at[at, :, 0:n], s_wd.at[j])
            wa[at, :, 0:n] = (pf[base : base + u, :, w:rows] + wd[at, :, 0:n].astype(F32)).astype(BF16)
            send(wa.at[at, :, 0:n], wr.at[to : to + u, :, 0:n], s_w.at[j], s_wr.at[k], south)

        @pl.when(dy == 3)
        def _():
            wait(wd.at[at, :, 0:n], s_wd.at[j])
            wa[at, :, 0:n] = (pf[base + u : base + 2 * u, :, w:rows] + wd[at, :, 0:n].astype(F32)).astype(BF16)
            send(wa.at[at, :, 0:n], wl.at[to + u : to + 2 * u, :, 0:n], s_w.at[j], s_wl.at[k], north)

    def y3(g, w, dy):
        _, to, u, base = wide(g)
        at, j, to1, k = parts(g)
        n = rows - w

        @pl.when(dy == 0)
        def _():
            wait(wl.at[to : to + 2 * u, :, 0:n], s_wl.at[k])
            wait(wr.at[to : to + 2 * u, :, 0:n], s_wr.at[k])

            @pl.loop(0, 2 * u)
            def _(i):
                summed = pf[base + i, :, w:rows] + wl[to + i, :, 0:n].astype(F32) + wr[to + i, :, 0:n].astype(F32)
                pf[base + i, :, w:rows] = summed
                p[base + i, :, w:rows] = summed.astype(BF16)

            exchange(g, w, (w + rows) // 2, rows, to1, k, vda, vdb, vl, vr, s_v, s_vda, s_vdb, s_vl, s_vr)

    def y4(g, w, dy):
        _, _, to, k = parts(g)

        @pl.when(dy == 0)
        def _():
            pass_on(g, w, (w + rows) // 2, rows, to, k, vda, vdb, vl, vr, va, s_v, s_vda, s_vdb, s_vl, s_vr)

    def y5(g, w, dy):
        _, _, to, k = parts(g)
        n = rows - w

        @pl.when(dy == 0)
        def _():
            wait(vl.at[to, :, 0:n], s_vl.at[k])
            wait(vr.at[to, :, 0:n], s_vr.at[k])
            total[to, :, w:rows] = (
                chunk(pf, g, x, w, rows)[...] + vl[to, :, 0:n].astype(F32) + vr[to, :, 0:n].astype(F32)
            )

    stages = {"x1": x1, "x2": x2_, "x3": x3, "x4": x4, "x5": x5, "y1": y1, "y2": y2, "y3": y3, "y4": y4, "y5": y5}
    loaded = []

    def compute(batch):
        groups = BATCHES[batch]
        for g in groups:
            wait(theirs(g), part.at[INDEX[g]])
        start, count = BASE[groups[0]], sum(4 * UNITS[k] for _, k in groups)
        unloaded = not loaded
        loaded.append(batch)

        @pl.loop(0, tiles)
        def _(t):
            if unloaded:
                weight(t).wait()
            left = diff[start : start + count].reshape(count * UNIT, diff.shape[-1])
            product = jnp.dot(left, weights[t], preferred_element_type=F32).reshape(count, UNIT, TILE)
            columns = pl.ds(pl.multiple_of(t * TILE, TILE), TILE)
            pf[start : start + count, :, columns] = product
            p[start : start + count, :, columns] = product.astype(BF16)

    for k in range(PIECES):
        to_partner((0, k))
        if k < AHEAD:
            ring_out(k)

    for step in SCHEDULE:
        name, n = step.split(".")[0], int(step.split(".")[1])
        if name == "f":
            forward(n)
        elif name == "r":
            far_end(n)
        elif name == "c":
            compute(n)
        else:
            for g in BATCHES[n]:
                stages[name](g, SPLIT[n], (y - z - g[0] + 8) % 4)

    for batch, groups in enumerate(BATCHES):
        w = SPLIT[batch]
        for s, k in groups:
            j, u = INDEX[s, k], UNITS[k]
            wait(diff.at[0 : (6, 3, 2, 3)[s] * u], ag_send.at[j])
            wait(p.at[0 : 3 * u, :, 0:w], s_x.at[j])

            @pl.when((y - z - s + 8) % 4 != 0)
            def _():
                wait(p.at[0:u, :, 0:w], s_z.at[j])
                wait(p.at[0 : 4 * u, :, w:rows], s_w.at[j])

            @pl.when((y - z - s + 8) % 4 == 0)
            def _():
                wait(p.at[0 : 3 * u, :, w:rows], s_v.at[k])


def shards(traces, features, nexts):
    tokens, rows = traces.shape
    groups = len(BASE)
    vmem, dma = pltpu.VMEM, pltpu.SemaphoreType.DMA
    of_groups, of_pieces = dma((groups,)), dma((PIECES,))
    scratch = [
        vmem(features.shape, BF16), vmem(features.shape, BF16),
        vmem((rows // TILE, tokens, TILE), BF16),
        vmem((16 * ALL, UNIT, tokens), BF16),
        vmem((16 * ALL, UNIT, rows), BF16), vmem((16 * ALL, UNIT, rows), F32),
        vmem((4 * ALL, UNIT, WX // 2), BF16), vmem((4 * ALL, UNIT, WX // 2), BF16),
        vmem((4 * ALL, UNIT, WX), BF16), vmem((4 * ALL, UNIT, WX), BF16), vmem((4 * ALL, UNIT, WX), BF16),
        vmem((4 * ALL, UNIT, WX // 2), BF16), vmem((4 * ALL, UNIT, WX // 2), BF16),
        vmem((ALL, UNIT, WX), BF16), vmem((ALL, UNIT, WX), BF16),
        vmem((8 * ALL, UNIT, WY), BF16), vmem((8 * ALL, UNIT, WY), BF16),
        vmem((4 * ALL, UNIT, WY), BF16), vmem((4 * ALL, UNIT, WY), BF16),
        vmem((ALL, UNIT, WY // 2), BF16), vmem((ALL, UNIT, WY // 2), BF16),
        vmem((ALL, UNIT, WY), BF16), vmem((ALL, UNIT, WY), BF16), vmem((ALL, UNIT, WY), BF16),
        dma((2 * CHUNKS,)), dma((rows // TILE,)), of_groups, of_groups, of_pieces, of_pieces, of_groups,
        of_groups, of_groups, of_groups, of_groups, of_groups,
        of_groups, of_pieces, of_pieces, of_groups,
        of_groups, of_pieces, of_pieces, of_groups,
        of_pieces, of_pieces, of_pieces, of_pieces, of_pieces,
    ]
    transposed = pl.pallas_call(
        kernel,
        out_shape=jax.ShapeDtypeStruct((ALL, UNIT, rows), F32),
        in_specs=[pl.BlockSpec(memory_space=pl.ANY)] * 3,
        out_specs=pl.BlockSpec(memory_space=pltpu.VMEM),
        scratch_shapes=scratch,
        compiler_params=pltpu.CompilerParams(
            collective_id=0, has_side_effects=True, vmem_limit_bytes=67043328
        ),
        name="panels",
    )(traces, features, nexts)
    return transposed.reshape(ALL * UNIT, rows).T


def solution(mesh):
    return jax.shard_map(
        shards,
        mesh=mesh,
        in_specs=(P(("col", "depth"), "row"), P(("col", "depth"), "row"), P(("col", "depth"), "row")),
        out_specs=P("row", ("col", "depth")),
        check_vma=False,
    )
```

```python
import jax
import jax.numpy as jnp
from jax import lax
from jax.experimental import pallas as pl
from jax.experimental.pallas import tpu as pltpu
from jax.sharding import PartitionSpec as P

DISCOUNT = 0.99
MESH = pl.DeviceIdType.MESH
F32, BF16 = jnp.float32, jnp.bfloat16
TILE = 512
CHUNKS = 4
UNIT = 16

UNITS = [2, 2, 2, 2]
AHEAD = 2
BATCHES = [
    [(0, 0)],
    [(0, 1)],
    [(0, 2)],
    [(0, 3)],
    [(1, 0)],
    [(3, 0)],
    [(1, 1)],
    [(3, 1)],
    [(2, 0)],
    [(1, 2)],
    [(3, 2)],
    [(2, 1)],
    [(1, 3)],
    [(3, 3)],
    [(2, 2)],
    [(2, 3)],
]
SPLIT = [1024, 1280, 1280, 1280, 1280, 1536, 1024, 1024, 1024, 1536, 1024, 1536, 1024, 1536, 1536, 1280]
SCHEDULE = [
    "c.0", "x1.0", "c.1", "x1.1", "d.0", "d.2", "d.3", "y1.3", "x2.0", "c.3", "x2.1", "x1.3", "y1.2", "f.0",
    "c.2", "x1.2", "y1.0", "d.1", "x3.1", "c.5", "x1.5", "c.4", "d.5", "f.1", "y1.1", "x1.4", "x2.2", "d.4",
    "y1.4", "x2.5", "y1.5", "d.7", "y1.7", "r.0", "d.6", "y1.6", "x2.4", "c.6", "x1.6", "c.7", "x1.7", "d.8",
    "y1.8", "y2.4", "c.8", "x1.8", "x2.6", "f.2", "y2.7", "x3.2", "x2.7", "x3.4", "x3.5", "y2.6", "y2.0", "x2.8",
    "c.10", "x1.10", "r.1", "y2.8", "c.9", "x1.9", "d.10", "y1.10", "x3.6", "c.11", "x1.11", "d.11", "y1.11", "x4.2",
    "x3.8", "x4.4", "x2.9", "x3.7", "f.3", "d.9", "y1.9", "y2.1", "x2.3", "x2.10", "x2.11", "y2.11", "y2.5", "x4.8",
    "y2.10", "r.2", "c.13", "x1.13", "x3.9", "c.12", "d.14", "y1.14", "x1.12", "r.3", "y3.8", "d.12", "y1.12", "x3.10",
    "c.14", "x1.14", "d.15", "y1.15", "d.13", "x2.13", "y1.13", "y2.3", "c.15", "x1.15", "y2.9", "y3.4", "y2.14", "x4.10",
    "x5.8", "x2.14", "x4.1", "x2.12", "x3.11", "y3.1", "y2.15", "y2.12", "y2.13", "y2.2", "x2.15", "y3.7", "x3.13", "y3.0",
    "y3.3", "x3.3", "y3.10", "y3.6", "y3.11", "x5.10", "x3.0", "x3.14", "x4.11", "y3.9", "x4.5", "y3.14", "x3.12", "y3.2",
    "x5.4", "y3.15", "y3.5", "y4.4", "y3.12", "x3.15", "y4.7", "x4.9", "x4.13", "y4.8", "x4.7", "y4.1", "x5.2", "y3.13",
    "x4.14", "y4.3", "x4.6", "y4.11", "x4.3", "y4.2", "y4.9", "x4.0", "y4.15", "y4.10", "y4.0", "y4.6", "x4.15", "y4.5",
    "x4.12", "y4.14", "y4.12", "y5.9", "y5.4", "x5.6", "y5.6", "y4.13", "x5.9", "x5.11", "x5.14", "y5.11", "y5.7", "y5.8",
    "x5.12", "y5.5", "x5.13", "x5.0", "y5.15", "y5.12", "y5.14", "x5.3", "y5.10", "y5.3", "x5.7", "y5.2", "y5.1", "x5.5",
    "x5.15", "y5.13", "x5.1", "y5.0",
]

PIECES = len(UNITS)
FIRST = [sum(UNITS[:k]) for k in range(PIECES + 1)]
BASE = {}
for _groups in BATCHES:
    for _s, _k in _groups:
        BASE[_s, _k] = sum(4 * UNITS[k] for s, k in BASE)
CHUNK = {g: BASE[g] // 4 for g in BASE}
INDEX = {g: i for i, g in enumerate(BASE)}
ALL = FIRST[-1]
WX, WY = max(SPLIT), 2048 - min(SPLIT)


def kernel(
    traces, features, nexts, out,
    feat, nxt, weights, diff, p, pf, total,
    xda, xdb, xl, xr, xa, zd, za, zl, zr, wd, wa, wl, wr, vda, vdb, vl, vr, va,
    load, load_t, leave, part, ring, ring_a, ring_b, ag_send,
    s_xda, s_xdb, s_xl, s_xr, s_x, s_zd, s_zl, s_zr, s_z, s_wd, s_wl, s_wr, s_w,
    s_vda, s_vdb, s_vl, s_vr, s_v,
):
    r, y, x = lax.axis_index("row"), lax.axis_index("col"), lax.axis_index("depth")
    z, h = r // 2, r % 2
    xp, xm, x2 = (x + 1) % 4, (x + 3) % 4, (x + 2) % 4
    east, west = {"depth": xp}, {"depth": xm}
    north, south = {"col": (y + 1) % 4}, {"col": (y + 3) % 4}
    up, down = {"row": (z + 1) % 4 * 2 + h}, {"row": (z + 3) % 4 * 2 + h}
    partner = {"row": z * 2 + 1 - h}
    rows = total.shape[-1]
    tiles = rows // TILE

    def send(src, dst, send_sem, recv_sem, where):
        pltpu.make_async_remote_copy(
            src_ref=src, dst_ref=dst, send_sem=send_sem, recv_sem=recv_sem, device_id=where, device_id_type=MESH
        ).start()

    def wait(ref, sem):
        pltpu.make_async_copy(ref, ref, sem).wait()

    tokens = feat.shape[0] // CHUNKS

    def loads(c):
        some = pl.ds(c * tokens, tokens)
        return [
            pltpu.make_async_copy(features.at[some], feat.at[some], load.at[c]),
            pltpu.make_async_copy(nexts.at[some], nxt.at[some], load.at[CHUNKS + c]),
        ]

    for c in range(CHUNKS):
        for copy in loads(c):
            copy.start()
    barrier = pltpu.get_barrier_semaphore()
    for where in (east, west, north, south, up, down, partner):
        pl.semaphore_signal(barrier, inc=1, device_id=where, device_id_type=MESH)

    def weight(t):
        some = pl.ds(t * TILE, TILE)
        return pltpu.make_async_copy(traces.at[:, some], weights.at[:, some], load_t.at[t])

    for c in range(CHUNKS):
        for copy in loads(c):
            copy.wait()
        if c == CHUNKS - 1:
            for t in range(tiles):
                weight(t).start()

        @pl.loop(c * tokens // 128, (c + 1) * tokens // 128)
        def _(t):
            some = pl.ds(pl.multiple_of(t * 128, 128), 128)
            d = feat[some, :].astype(F32) - DISCOUNT * nxt[some, :].astype(F32)
            d = d.astype(BF16).T.reshape(2, ALL, UNIT, 128)
            for b in range(2):
                for k in range(PIECES):
                    u = UNITS[k]
                    diff[pl.ds(BASE[0, k] + (2 * h + b) * u, u), :, some] = d[b, FIRST[k] : FIRST[k] + u]

    pl.semaphore_wait(barrier, 7)


    def mine(g):
        u = UNITS[g[1]]
        return diff.at[pl.ds(BASE[g] + 2 * h * u, 2 * u)]

    def theirs(g):
        u = UNITS[g[1]]
        return diff.at[pl.ds(BASE[g] + 2 * (1 - h) * u, 2 * u)]

    def one(g, b):
        u = UNITS[g[1]]
        return diff.at[pl.ds(BASE[g] + (2 * h + b) * u, u)]

    def ring_out(k):
        if k >= PIECES:
            return
        send(mine((0, k)), mine((3, k)), ag_send.at[INDEX[0, k]], ring.at[INDEX[3, k]], up)
        send(mine((0, k)), mine((1, k)), ag_send.at[INDEX[0, k]], ring.at[INDEX[1, k]], down)

    def to_partner(g):
        send(mine(g), mine(g), ag_send.at[INDEX[g]], part.at[INDEX[g]], partner)

    def forward(k):
        below, above, far = (3, k), (1, k), (2, k)
        wait(mine(below), ring.at[INDEX[below]])
        send(one(below, 0), one(far, 0), ag_send.at[INDEX[below]], ring_a.at[k], up)
        wait(mine(above), ring.at[INDEX[above]])
        send(one(above, 1), one(far, 1), ag_send.at[INDEX[above]], ring_b.at[k], down)
        ring_out(k + AHEAD)
        to_partner(below)
        to_partner(above)

    def far_end(k):
        far = (2, k)
        wait(one(far, 0), ring_a.at[k])
        wait(one(far, 1), ring_b.at[k])
        to_partner(far)


    def chunk(ref, g, i, lo, hi):
        u = UNITS[g[1]]
        return ref.at[pl.ds(BASE[g] + i * u, u), :, lo:hi]

    def exchange(g, lo, mid, hi, at, j, da, db, left, right, sends, s_da, s_db, s_l, s_r):
        n = mid - lo
        send(chunk(p, g, x2, lo, mid), da.at[at, :, 0:n], sends.at[j], s_da.at[j], east)
        send(chunk(p, g, x2, mid, hi), db.at[at, :, 0:n], sends.at[j], s_db.at[j], west)
        send(chunk(p, g, xp, mid, hi), left.at[at, :, n : 2 * n], sends.at[j], s_l.at[j], east)
        send(chunk(p, g, xm, lo, mid), right.at[at, :, 0:n], sends.at[j], s_r.at[j], west)

    def pass_on(g, lo, mid, hi, at, j, da, db, left, right, acc, sends, s_da, s_db, s_l, s_r):
        n = mid - lo
        wait(da.at[at, :, 0:n], s_da.at[j])
        acc[at, :, 0:n] = (chunk(pf, g, xp, lo, mid)[...] + da[at, :, 0:n].astype(F32)).astype(BF16)
        send(acc.at[at, :, 0:n], left.at[at, :, 0:n], sends.at[j], s_l.at[j], east)
        wait(db.at[at, :, 0:n], s_db.at[j])
        acc[at, :, n : 2 * n] = (chunk(pf, g, xm, mid, hi)[...] + db[at, :, 0:n].astype(F32)).astype(BF16)
        send(acc.at[at, :, n : 2 * n], right.at[at, :, n : 2 * n], sends.at[j], s_r.at[j], west)

    def parts(g):
        u = UNITS[g[1]]
        return pl.ds(CHUNK[g], u), INDEX[g], pl.ds(FIRST[g[1]], u), g[1]

    def x1(g, w, dy):
        at, j, _, _ = parts(g)
        exchange(g, 0, w // 2, w, at, j, xda, xdb, xl, xr, s_x, s_xda, s_xdb, s_xl, s_xr)

    def x2_(g, w, dy):
        at, j, _, _ = parts(g)
        pass_on(g, 0, w // 2, w, at, j, xda, xdb, xl, xr, xa, s_x, s_xda, s_xdb, s_xl, s_xr)

    def x3(g, w, dy):
        at, j, to, k = parts(g)
        n = w // 2
        wait(xl.at[at, :, 0:w], s_xl.at[j])
        wait(xr.at[at, :, 0:w], s_xr.at[j])
        own = chunk(pf, g, x, 0, w)
        summed = own[...] + xl[at, :, 0:w].astype(F32) + xr[at, :, 0:w].astype(F32)

        @pl.when(dy == 0)
        def _():
            total[to, :, 0:w] = summed

        @pl.when(dy != 0)
        def _():
            own[...] = summed
            chunk(p, g, x, 0, w)[...] = summed.astype(BF16)

        a, b = chunk(p, g, x, 0, n), chunk(p, g, x, n, w)

        @pl.when(dy == 2)
        def _():
            send(a, zd.at[at, :, 0:n], s_z.at[j], s_zd.at[j], south)
            send(b, zd.at[at, :, 0:n], s_z.at[j], s_zd.at[j], north)

        @pl.when(dy == 1)
        def _():
            send(b, zr.at[to, :, n:w], s_z.at[j], s_zr.at[k], south)

        @pl.when(dy == 3)
        def _():
            send(a, zl.at[to, :, 0:n], s_z.at[j], s_zl.at[k], north)

    def x4(g, w, dy):
        at, j, to, k = parts(g)
        n = w // 2

        @pl.when(dy == 1)
        def _():
            wait(zd.at[at, :, 0:n], s_zd.at[j])
            za[at, :, 0:n] = (chunk(pf, g, x, 0, n)[...] + zd[at, :, 0:n].astype(F32)).astype(BF16)
            send(za.at[at, :, 0:n], zr.at[to, :, 0:n], s_z.at[j], s_zr.at[k], south)

        @pl.when(dy == 3)
        def _():
            wait(zd.at[at, :, 0:n], s_zd.at[j])
            za[at, :, 0:n] = (chunk(pf, g, x, n, w)[...] + zd[at, :, 0:n].astype(F32)).astype(BF16)
            send(za.at[at, :, 0:n], zl.at[to, :, n:w], s_z.at[j], s_zl.at[k], north)

    def result(k, lo, hi, j):
        to = pl.ds(FIRST[k], UNITS[k])
        return pltpu.make_async_copy(total.at[to, :, lo:hi], out.at[to, :, lo:hi], leave.at[j])

    def x5(g, w, dy):
        _, _, to, k = parts(g)

        @pl.when(dy == 0)
        def _():
            wait(zl.at[to, :, 0:w], s_zl.at[k])
            wait(zr.at[to, :, 0:w], s_zr.at[k])
            total[to, :, 0:w] += zl[to, :, 0:w].astype(F32) + zr[to, :, 0:w].astype(F32)
            result(k, 0, w, 2 * k).start()

    def wide(g):
        u = UNITS[g[1]]
        return pl.ds(2 * CHUNK[g], 2 * u), 4 * FIRST[g[1]], 2 * u, BASE[g]

    def y1(g, w, dy):
        at, to, u, base = wide(g)
        _, j, _, k = parts(g)
        n = rows - w
        a, b = p.at[base : base + u, :, w:rows], p.at[base + u : base + 2 * u, :, w:rows]

        @pl.when(dy == 2)
        def _():
            send(a, wd.at[at, :, 0:n], s_w.at[j], s_wd.at[j], south)
            send(b, wd.at[at, :, 0:n], s_w.at[j], s_wd.at[j], north)

        @pl.when(dy == 1)
        def _():
            send(b, wr.at[to + u : to + 2 * u, :, 0:n], s_w.at[j], s_wr.at[k], south)

        @pl.when(dy == 3)
        def _():
            send(a, wl.at[to : to + u, :, 0:n], s_w.at[j], s_wl.at[k], north)

    def y2(g, w, dy):
        at, to, u, base = wide(g)
        _, j, _, k = parts(g)
        n = rows - w

        @pl.when(dy == 1)
        def _():
            wait(wd.at[at, :, 0:n], s_wd.at[j])
            wa[at, :, 0:n] = (pf[base : base + u, :, w:rows] + wd[at, :, 0:n].astype(F32)).astype(BF16)
            send(wa.at[at, :, 0:n], wr.at[to : to + u, :, 0:n], s_w.at[j], s_wr.at[k], south)

        @pl.when(dy == 3)
        def _():
            wait(wd.at[at, :, 0:n], s_wd.at[j])
            wa[at, :, 0:n] = (pf[base + u : base + 2 * u, :, w:rows] + wd[at, :, 0:n].astype(F32)).astype(BF16)
            send(wa.at[at, :, 0:n], wl.at[to + u : to + 2 * u, :, 0:n], s_w.at[j], s_wl.at[k], north)

    def y3(g, w, dy):
        _, to, u, base = wide(g)
        at, j, to1, k = parts(g)
        n = rows - w

        @pl.when(dy == 0)
        def _():
            wait(wl.at[to : to + 2 * u, :, 0:n], s_wl.at[k])
            wait(wr.at[to : to + 2 * u, :, 0:n], s_wr.at[k])

            @pl.loop(0, 2 * u)
            def _(i):
                summed = pf[base + i, :, w:rows] + wl[to + i, :, 0:n].astype(F32) + wr[to + i, :, 0:n].astype(F32)
                pf[base + i, :, w:rows] = summed
                p[base + i, :, w:rows] = summed.astype(BF16)

            exchange(g, w, (w + rows) // 2, rows, to1, k, vda, vdb, vl, vr, s_v, s_vda, s_vdb, s_vl, s_vr)

    def y4(g, w, dy):
        _, _, to, k = parts(g)

        @pl.when(dy == 0)
        def _():
            pass_on(g, w, (w + rows) // 2, rows, to, k, vda, vdb, vl, vr, va, s_v, s_vda, s_vdb, s_vl, s_vr)

    def y5(g, w, dy):
        _, _, to, k = parts(g)
        n = rows - w

        @pl.when(dy == 0)
        def _():
            wait(vl.at[to, :, 0:n], s_vl.at[k])
            wait(vr.at[to, :, 0:n], s_vr.at[k])
            total[to, :, w:rows] = (
                chunk(pf, g, x, w, rows)[...] + vl[to, :, 0:n].astype(F32) + vr[to, :, 0:n].astype(F32)
            )
            result(k, w, rows, 2 * k + 1).start()

    stages = {"x1": x1, "x2": x2_, "x3": x3, "x4": x4, "x5": x5, "y1": y1, "y2": y2, "y3": y3, "y4": y4, "y5": y5}
    waited = set()

    def once(what, waiting):
        if what not in waited:
            waited.add(what)
            waiting()

    def compute(batch, lo, hi):
        groups = BATCHES[batch]
        for g in groups:
            once(g, lambda g=g: wait(theirs(g), part.at[INDEX[g]]))
        for t in range(lo // TILE, -(-hi // TILE)):
            once(t, lambda t=t: weight(t).wait())
        start, count = BASE[groups[0]], sum(4 * UNITS[k] for _, k in groups)
        left = diff[start : start + count].reshape(count * UNIT, diff.shape[-1])
        product = jnp.dot(left, weights[:, lo:hi], preferred_element_type=F32).reshape(count, UNIT, hi - lo)
        pf[start : start + count, :, lo:hi] = product
        p[start : start + count, :, lo:hi] = product.astype(BF16)

    for k in range(PIECES):
        to_partner((0, k))
        if k < AHEAD:
            ring_out(k)

    for step in SCHEDULE:
        name, n = step.split(".")[0], int(step.split(".")[1])
        if name == "f":
            forward(n)
        elif name == "r":
            far_end(n)
        elif name == "c":
            compute(n, 0, SPLIT[n])
        elif name == "d":
            compute(n, SPLIT[n], rows)
        else:
            for g in BATCHES[n]:
                stages[name](g, SPLIT[n], (y - z - g[0] + 8) % 4)

    for batch, groups in enumerate(BATCHES):
        w = SPLIT[batch]
        for s, k in groups:
            j, u = INDEX[s, k], UNITS[k]
            wait(diff.at[0 : (6, 3, 2, 3)[s] * u], ag_send.at[j])
            wait(p.at[0 : 3 * u, :, 0:w], s_x.at[j])

            @pl.when((y - z - s + 8) % 4 != 0)
            def _():
                wait(p.at[0:u, :, 0:w], s_z.at[j])
                wait(p.at[0 : 4 * u, :, w:rows], s_w.at[j])

            @pl.when((y - z - s + 8) % 4 == 0)
            def _():
                wait(p.at[0 : 3 * u, :, w:rows], s_v.at[k])
                result(k, 0, w, 2 * k).wait()
                result(k, w, rows, 2 * k + 1).wait()


def shards(traces, features, nexts):
    tokens, rows = traces.shape
    groups = len(BASE)
    vmem, dma = pltpu.VMEM, pltpu.SemaphoreType.DMA
    of_groups, of_pieces = dma((groups,)), dma((PIECES,))
    scratch = [
        vmem(features.shape, BF16), vmem(features.shape, BF16),
        vmem(traces.shape, BF16),
        vmem((16 * ALL, UNIT, tokens), BF16),
        vmem((16 * ALL, UNIT, rows), BF16), vmem((16 * ALL, UNIT, rows), F32),
        vmem((ALL, UNIT, rows), F32),
        vmem((4 * ALL, UNIT, WX // 2), BF16), vmem((4 * ALL, UNIT, WX // 2), BF16),
        vmem((4 * ALL, UNIT, WX), BF16), vmem((4 * ALL, UNIT, WX), BF16), vmem((4 * ALL, UNIT, WX), BF16),
        vmem((4 * ALL, UNIT, WX // 2), BF16), vmem((4 * ALL, UNIT, WX // 2), BF16),
        vmem((ALL, UNIT, WX), BF16), vmem((ALL, UNIT, WX), BF16),
        vmem((8 * ALL, UNIT, WY), BF16), vmem((8 * ALL, UNIT, WY), BF16),
        vmem((4 * ALL, UNIT, WY), BF16), vmem((4 * ALL, UNIT, WY), BF16),
        vmem((ALL, UNIT, WY // 2), BF16), vmem((ALL, UNIT, WY // 2), BF16),
        vmem((ALL, UNIT, WY), BF16), vmem((ALL, UNIT, WY), BF16), vmem((ALL, UNIT, WY), BF16),
        dma((2 * CHUNKS,)), dma((rows // TILE,)), dma((2 * PIECES,)), of_groups, of_groups, of_pieces, of_pieces, of_groups,
        of_groups, of_groups, of_groups, of_groups, of_groups,
        of_groups, of_pieces, of_pieces, of_groups,
        of_groups, of_pieces, of_pieces, of_groups,
        of_pieces, of_pieces, of_pieces, of_pieces, of_pieces,
    ]
    transposed = pl.pallas_call(
        kernel,
        out_shape=jax.ShapeDtypeStruct((ALL, UNIT, rows), F32),
        in_specs=[pl.BlockSpec(memory_space=pl.ANY)] * 3,
        out_specs=pl.BlockSpec(memory_space=pl.ANY),
        scratch_shapes=scratch,
        compiler_params=pltpu.CompilerParams(
            collective_id=0, has_side_effects=True, vmem_limit_bytes=67043328
        ),
        name="panels",
    )(traces, features, nexts)
    return transposed.reshape(ALL * UNIT, rows).T


def solution(mesh):
    return jax.shard_map(
        shards,
        mesh=mesh,
        in_specs=(P(("col", "depth"), "row"), P(("col", "depth"), "row"), P(("col", "depth"), "row")),
        out_specs=P("row", ("col", "depth")),
        check_vma=False,
    )
```

```python
import jax
import jax.numpy as jnp
from jax import lax
from jax.experimental import pallas as pl
from jax.experimental.pallas import tpu as pltpu
from jax.sharding import PartitionSpec as P

DISCOUNT = 0.99
MESH = pl.DeviceIdType.MESH
F32, BF16 = jnp.float32, jnp.bfloat16
TILE = 512
CHUNKS = 4
UNIT = 16

UNITS = [2, 2, 2, 2]
AHEAD = 2
BATCHES = [
    [(0, 0)],
    [(0, 1)],
    [(0, 2)],
    [(0, 3)],
    [(1, 0)],
    [(3, 0)],
    [(1, 1)],
    [(3, 1)],
    [(2, 0)],
    [(1, 2)],
    [(3, 2)],
    [(2, 1)],
    [(1, 3)],
    [(3, 3)],
    [(2, 2)],
    [(2, 3)],
]
SPLIT = [1024, 1280, 1280, 1280, 1280, 1536, 1024, 1024, 1024, 1536, 1024, 1536, 1024, 1536, 1536, 1280]
SCHEDULE = [
    "c.0", "x1.0", "c.1", "x1.1", "d.0", "d.2", "d.3", "y1.3", "x2.0", "c.3", "x2.1", "x1.3", "y1.2", "f.0",
    "c.2", "x1.2", "y1.0", "d.1", "x3.1", "c.5", "x1.5", "c.4", "d.5", "f.1", "y1.1", "x1.4", "x2.2", "d.4",
    "y1.4", "x2.5", "y1.5", "d.7", "y1.7", "r.0", "d.6", "y1.6", "x2.4", "c.6", "x1.6", "c.7", "x1.7", "d.8",
    "y1.8", "y2.4", "c.8", "x1.8", "x2.6", "f.2", "y2.7", "x3.2", "x2.7", "x3.4", "x3.5", "y2.6", "y2.0", "x2.8",
    "c.10", "x1.10", "r.1", "y2.8", "c.9", "x1.9", "d.10", "y1.10", "x3.6", "c.11", "x1.11", "d.11", "y1.11", "x4.2",
    "x3.8", "x4.4", "x2.9", "x3.7", "f.3", "d.9", "y1.9", "y2.1", "x2.3", "x2.10", "x2.11", "y2.11", "y2.5", "x4.8",
    "y2.10", "r.2", "c.13", "x1.13", "x3.9", "c.12", "d.14", "y1.14", "x1.12", "r.3", "y3.8", "d.12", "y1.12", "x3.10",
    "c.14", "x1.14", "d.15", "y1.15", "d.13", "x2.13", "y1.13", "y2.3", "c.15", "x1.15", "y2.9", "y3.4", "y2.14", "x4.10",
    "x5.8", "x2.14", "x4.1", "x2.12", "x3.11", "y3.1", "y2.15", "y2.12", "y2.13", "y2.2", "x2.15", "y3.7", "x3.13", "y3.0",
    "y3.3", "x3.3", "y3.10", "y3.6", "y3.11", "x5.10", "x3.0", "x3.14", "x4.11", "y3.9", "x4.5", "y3.14", "x3.12", "y3.2",
    "x5.4", "y3.15", "y3.5", "y4.4", "y3.12", "x3.15", "y4.7", "x4.9", "x4.13", "y4.8", "x4.7", "y4.1", "x5.2", "y3.13",
    "x4.14", "y4.3", "x4.6", "y4.11", "x4.3", "y4.2", "y4.9", "x4.0", "y4.15", "y4.10", "y4.0", "y4.6", "x4.15", "y4.5",
    "x4.12", "y4.14", "y4.12", "y5.9", "y5.4", "x5.6", "y5.6", "y4.13", "x5.9", "x5.11", "x5.14", "y5.11", "y5.7", "y5.8",
    "x5.12", "y5.5", "x5.13", "x5.0", "y5.15", "y5.12", "y5.14", "x5.3", "y5.10", "y5.3", "x5.7", "y5.2", "y5.1", "x5.5",
    "x5.15", "y5.13", "x5.1", "y5.0",
]

PIECES = len(UNITS)
FIRST = [sum(UNITS[:k]) for k in range(PIECES + 1)]
BASE = {}
for _groups in BATCHES:
    for _s, _k in _groups:
        BASE[_s, _k] = sum(4 * UNITS[k] for s, k in BASE)
CHUNK = {g: BASE[g] // 4 for g in BASE}
INDEX = {g: i for i, g in enumerate(BASE)}
ALL = FIRST[-1]
WX, WY = max(SPLIT), 2048 - min(SPLIT)


def kernel(
    traces, features, nexts, out,
    feat, nxt, weights, diff, p, pf, total,
    xda, xdb, xl, xr, xa, zd, za, zl, zr, wd, wa, wl, wr, vda, vdb, vl, vr, va,
    load, load_t, leave, part, ring, ring_a, ring_b, ag_send,
    s_xda, s_xdb, s_xl, s_xr, s_x, s_zd, s_zl, s_zr, s_z, s_wd, s_wl, s_wr, s_w,
    s_vda, s_vdb, s_vl, s_vr, s_v,
):
    r, y, x = lax.axis_index("row"), lax.axis_index("col"), lax.axis_index("depth")
    z, h = r // 2, r % 2
    xp, xm, x2 = (x + 1) % 4, (x + 3) % 4, (x + 2) % 4
    east, west = {"depth": xp}, {"depth": xm}
    north, south = {"col": (y + 1) % 4}, {"col": (y + 3) % 4}
    up, down = {"row": (z + 1) % 4 * 2 + h}, {"row": (z + 3) % 4 * 2 + h}
    partner = {"row": z * 2 + 1 - h}
    rows = total.shape[-1]
    tiles = rows // TILE

    def send(src, dst, send_sem, recv_sem, where):
        pltpu.make_async_remote_copy(
            src_ref=src, dst_ref=dst, send_sem=send_sem, recv_sem=recv_sem, device_id=where, device_id_type=MESH
        ).start()

    def wait(ref, sem):
        pltpu.make_async_copy(ref, ref, sem).wait()

    tokens = feat.shape[0] // CHUNKS

    def loads(c):
        some = pl.ds(c * tokens, tokens)
        return [
            pltpu.make_async_copy(features.at[some], feat.at[some], load.at[c]),
            pltpu.make_async_copy(nexts.at[some], nxt.at[some], load.at[CHUNKS + c]),
        ]

    barrier = pltpu.get_barrier_semaphore()
    for where in (east, west, north, south, up, down, partner):
        pl.semaphore_signal(barrier, inc=1, device_id=where, device_id_type=MESH)
    for c in range(CHUNKS):
        for copy in loads(c):
            copy.start()

    def weight(t):
        some = pl.ds(t * TILE, TILE)
        return pltpu.make_async_copy(traces.at[:, some], weights.at[:, some], load_t.at[t])

    for c in range(CHUNKS):
        for copy in loads(c):
            copy.wait()
        if c == CHUNKS - 1:
            for t in range(tiles):
                weight(t).start()

        @pl.loop(c * tokens // 128, (c + 1) * tokens // 128)
        def _(t):
            some = pl.ds(pl.multiple_of(t * 128, 128), 128)
            d = feat[some, :].astype(F32) - DISCOUNT * nxt[some, :].astype(F32)
            d = d.astype(BF16).T.reshape(2, ALL, UNIT, 128)
            for b in range(2):
                for k in range(PIECES):
                    u = UNITS[k]
                    diff[pl.ds(BASE[0, k] + (2 * h + b) * u, u), :, some] = d[b, FIRST[k] : FIRST[k] + u]

    pl.semaphore_wait(barrier, 7)


    def mine(g):
        u = UNITS[g[1]]
        return diff.at[pl.ds(BASE[g] + 2 * h * u, 2 * u)]

    def theirs(g):
        u = UNITS[g[1]]
        return diff.at[pl.ds(BASE[g] + 2 * (1 - h) * u, 2 * u)]

    def one(g, b):
        u = UNITS[g[1]]
        return diff.at[pl.ds(BASE[g] + (2 * h + b) * u, u)]

    def ring_out(k):
        if k >= PIECES:
            return
        send(mine((0, k)), mine((3, k)), ag_send.at[INDEX[0, k]], ring.at[INDEX[3, k]], up)
        send(mine((0, k)), mine((1, k)), ag_send.at[INDEX[0, k]], ring.at[INDEX[1, k]], down)

    def to_partner(g):
        send(mine(g), mine(g), ag_send.at[INDEX[g]], part.at[INDEX[g]], partner)

    def forward(k):
        below, above, far = (3, k), (1, k), (2, k)
        wait(mine(below), ring.at[INDEX[below]])
        send(one(below, 0), one(far, 0), ag_send.at[INDEX[below]], ring_a.at[k], up)
        wait(mine(above), ring.at[INDEX[above]])
        send(one(above, 1), one(far, 1), ag_send.at[INDEX[above]], ring_b.at[k], down)
        ring_out(k + AHEAD)
        to_partner(below)
        to_partner(above)

    def far_end(k):
        far = (2, k)
        wait(one(far, 0), ring_a.at[k])
        wait(one(far, 1), ring_b.at[k])
        to_partner(far)


    def chunk(ref, g, i, lo, hi):
        u = UNITS[g[1]]
        return ref.at[pl.ds(BASE[g] + i * u, u), :, lo:hi]

    def exchange(g, lo, mid, hi, at, j, da, db, left, right, sends, s_da, s_db, s_l, s_r):
        n = mid - lo
        send(chunk(p, g, x2, lo, mid), da.at[at, :, 0:n], sends.at[j], s_da.at[j], east)
        send(chunk(p, g, x2, mid, hi), db.at[at, :, 0:n], sends.at[j], s_db.at[j], west)
        send(chunk(p, g, xp, mid, hi), left.at[at, :, n : 2 * n], sends.at[j], s_l.at[j], east)
        send(chunk(p, g, xm, lo, mid), right.at[at, :, 0:n], sends.at[j], s_r.at[j], west)

    def pass_on(g, lo, mid, hi, at, j, da, db, left, right, acc, sends, s_da, s_db, s_l, s_r):
        n = mid - lo
        wait(da.at[at, :, 0:n], s_da.at[j])
        acc[at, :, 0:n] = (chunk(pf, g, xp, lo, mid)[...] + da[at, :, 0:n].astype(F32)).astype(BF16)
        send(acc.at[at, :, 0:n], left.at[at, :, 0:n], sends.at[j], s_l.at[j], east)
        wait(db.at[at, :, 0:n], s_db.at[j])
        acc[at, :, n : 2 * n] = (chunk(pf, g, xm, mid, hi)[...] + db[at, :, 0:n].astype(F32)).astype(BF16)
        send(acc.at[at, :, n : 2 * n], right.at[at, :, n : 2 * n], sends.at[j], s_r.at[j], west)

    def parts(g):
        u = UNITS[g[1]]
        return pl.ds(CHUNK[g], u), INDEX[g], pl.ds(FIRST[g[1]], u), g[1]

    def x1(g, w, dy):
        at, j, _, _ = parts(g)
        exchange(g, 0, w // 2, w, at, j, xda, xdb, xl, xr, s_x, s_xda, s_xdb, s_xl, s_xr)

    def x2_(g, w, dy):
        at, j, _, _ = parts(g)
        pass_on(g, 0, w // 2, w, at, j, xda, xdb, xl, xr, xa, s_x, s_xda, s_xdb, s_xl, s_xr)

    def x3(g, w, dy):
        at, j, to, k = parts(g)
        n = w // 2
        wait(xl.at[at, :, 0:w], s_xl.at[j])
        wait(xr.at[at, :, 0:w], s_xr.at[j])
        own = chunk(pf, g, x, 0, w)
        summed = own[...] + xl[at, :, 0:w].astype(F32) + xr[at, :, 0:w].astype(F32)

        @pl.when(dy == 0)
        def _():
            total[to, :, 0:w] = summed

        @pl.when(dy != 0)
        def _():
            own[...] = summed
            chunk(p, g, x, 0, w)[...] = summed.astype(BF16)

        a, b = chunk(p, g, x, 0, n), chunk(p, g, x, n, w)

        @pl.when(dy == 2)
        def _():
            send(a, zd.at[at, :, 0:n], s_z.at[j], s_zd.at[j], south)
            send(b, zd.at[at, :, 0:n], s_z.at[j], s_zd.at[j], north)

        @pl.when(dy == 1)
        def _():
            send(b, zr.at[to, :, n:w], s_z.at[j], s_zr.at[k], south)

        @pl.when(dy == 3)
        def _():
            send(a, zl.at[to, :, 0:n], s_z.at[j], s_zl.at[k], north)

    def x4(g, w, dy):
        at, j, to, k = parts(g)
        n = w // 2

        @pl.when(dy == 1)
        def _():
            wait(zd.at[at, :, 0:n], s_zd.at[j])
            za[at, :, 0:n] = (chunk(pf, g, x, 0, n)[...] + zd[at, :, 0:n].astype(F32)).astype(BF16)
            send(za.at[at, :, 0:n], zr.at[to, :, 0:n], s_z.at[j], s_zr.at[k], south)

        @pl.when(dy == 3)
        def _():
            wait(zd.at[at, :, 0:n], s_zd.at[j])
            za[at, :, 0:n] = (chunk(pf, g, x, n, w)[...] + zd[at, :, 0:n].astype(F32)).astype(BF16)
            send(za.at[at, :, 0:n], zl.at[to, :, n:w], s_z.at[j], s_zl.at[k], north)

    def result(k, lo, hi, j):
        to = pl.ds(FIRST[k], UNITS[k])
        return pltpu.make_async_copy(total.at[to, :, lo:hi], out.at[to, :, lo:hi], leave.at[j])

    def x5(g, w, dy):
        _, _, to, k = parts(g)

        @pl.when(dy == 0)
        def _():
            wait(zl.at[to, :, 0:w], s_zl.at[k])
            wait(zr.at[to, :, 0:w], s_zr.at[k])
            total[to, :, 0:w] += zl[to, :, 0:w].astype(F32) + zr[to, :, 0:w].astype(F32)
            result(k, 0, w, 2 * k).start()

    def wide(g):
        u = UNITS[g[1]]
        return pl.ds(2 * CHUNK[g], 2 * u), 4 * FIRST[g[1]], 2 * u, BASE[g]

    def y1(g, w, dy):
        at, to, u, base = wide(g)
        _, j, _, k = parts(g)
        n = rows - w
        a, b = p.at[base : base + u, :, w:rows], p.at[base + u : base + 2 * u, :, w:rows]

        @pl.when(dy == 2)
        def _():
            send(a, wd.at[at, :, 0:n], s_w.at[j], s_wd.at[j], south)
            send(b, wd.at[at, :, 0:n], s_w.at[j], s_wd.at[j], north)

        @pl.when(dy == 1)
        def _():
            send(b, wr.at[to + u : to + 2 * u, :, 0:n], s_w.at[j], s_wr.at[k], south)

        @pl.when(dy == 3)
        def _():
            send(a, wl.at[to : to + u, :, 0:n], s_w.at[j], s_wl.at[k], north)

    def y2(g, w, dy):
        at, to, u, base = wide(g)
        _, j, _, k = parts(g)
        n = rows - w

        @pl.when(dy == 1)
        def _():
            wait(wd.at[at, :, 0:n], s_wd.at[j])
            wa[at, :, 0:n] = (pf[base : base + u, :, w:rows] + wd[at, :, 0:n].astype(F32)).astype(BF16)
            send(wa.at[at, :, 0:n], wr.at[to : to + u, :, 0:n], s_w.at[j], s_wr.at[k], south)

        @pl.when(dy == 3)
        def _():
            wait(wd.at[at, :, 0:n], s_wd.at[j])
            wa[at, :, 0:n] = (pf[base + u : base + 2 * u, :, w:rows] + wd[at, :, 0:n].astype(F32)).astype(BF16)
            send(wa.at[at, :, 0:n], wl.at[to + u : to + 2 * u, :, 0:n], s_w.at[j], s_wl.at[k], north)

    def y3(g, w, dy):
        _, to, u, base = wide(g)
        at, j, to1, k = parts(g)
        n = rows - w

        @pl.when(dy == 0)
        def _():
            wait(wl.at[to : to + 2 * u, :, 0:n], s_wl.at[k])
            wait(wr.at[to : to + 2 * u, :, 0:n], s_wr.at[k])

            @pl.loop(0, 2 * u)
            def _(i):
                summed = pf[base + i, :, w:rows] + wl[to + i, :, 0:n].astype(F32) + wr[to + i, :, 0:n].astype(F32)
                pf[base + i, :, w:rows] = summed
                p[base + i, :, w:rows] = summed.astype(BF16)

            exchange(g, w, (w + rows) // 2, rows, to1, k, vda, vdb, vl, vr, s_v, s_vda, s_vdb, s_vl, s_vr)

    def y4(g, w, dy):
        _, _, to, k = parts(g)

        @pl.when(dy == 0)
        def _():
            pass_on(g, w, (w + rows) // 2, rows, to, k, vda, vdb, vl, vr, va, s_v, s_vda, s_vdb, s_vl, s_vr)

    def y5(g, w, dy):
        _, _, to, k = parts(g)
        n = rows - w

        @pl.when(dy == 0)
        def _():
            wait(vl.at[to, :, 0:n], s_vl.at[k])
            wait(vr.at[to, :, 0:n], s_vr.at[k])
            total[to, :, w:rows] = (
                chunk(pf, g, x, w, rows)[...] + vl[to, :, 0:n].astype(F32) + vr[to, :, 0:n].astype(F32)
            )
            result(k, w, rows, 2 * k + 1).start()

    stages = {"x1": x1, "x2": x2_, "x3": x3, "x4": x4, "x5": x5, "y1": y1, "y2": y2, "y3": y3, "y4": y4, "y5": y5}
    waited = set()

    def once(what, waiting):
        if what not in waited:
            waited.add(what)
            waiting()

    def compute(batch, lo, hi):
        groups = BATCHES[batch]
        for g in groups:
            once(g, lambda g=g: wait(theirs(g), part.at[INDEX[g]]))
        for t in range(lo // TILE, -(-hi // TILE)):
            once(t, lambda t=t: weight(t).wait())
        start, count = BASE[groups[0]], sum(4 * UNITS[k] for _, k in groups)
        left = diff[start : start + count].reshape(count * UNIT, diff.shape[-1])
        product = jnp.dot(left, weights[:, lo:hi], preferred_element_type=F32).reshape(count, UNIT, hi - lo)
        pf[start : start + count, :, lo:hi] = product
        p[start : start + count, :, lo:hi] = product.astype(BF16)

    for k in range(PIECES):
        to_partner((0, k))
        if k < AHEAD:
            ring_out(k)

    for step in SCHEDULE:
        name, n = step.split(".")[0], int(step.split(".")[1])
        if name == "f":
            forward(n)
        elif name == "r":
            far_end(n)
        elif name == "c":
            compute(n, 0, SPLIT[n])
        elif name == "d":
            compute(n, SPLIT[n], rows)
        else:
            for g in BATCHES[n]:
                stages[name](g, SPLIT[n], (y - z - g[0] + 8) % 4)

    for batch, groups in enumerate(BATCHES):
        w = SPLIT[batch]
        for s, k in groups:
            j, u = INDEX[s, k], UNITS[k]
            wait(diff.at[0 : (6, 3, 2, 3)[s] * u], ag_send.at[j])
            wait(p.at[0 : 3 * u, :, 0:w], s_x.at[j])

            @pl.when((y - z - s + 8) % 4 != 0)
            def _():
                wait(p.at[0:u, :, 0:w], s_z.at[j])
                wait(p.at[0 : 4 * u, :, w:rows], s_w.at[j])

            @pl.when((y - z - s + 8) % 4 == 0)
            def _():
                wait(p.at[0 : 3 * u, :, w:rows], s_v.at[k])
                result(k, 0, w, 2 * k).wait()
                result(k, w, rows, 2 * k + 1).wait()


def shards(traces, features, nexts):
    tokens, rows = traces.shape
    groups = len(BASE)
    vmem, dma = pltpu.VMEM, pltpu.SemaphoreType.DMA
    of_groups, of_pieces = dma((groups,)), dma((PIECES,))
    scratch = [
        vmem(features.shape, BF16), vmem(features.shape, BF16),
        vmem(traces.shape, BF16),
        vmem((16 * ALL, UNIT, tokens), BF16),
        vmem((16 * ALL, UNIT, rows), BF16), vmem((16 * ALL, UNIT, rows), F32),
        vmem((ALL, UNIT, rows), F32),
        vmem((4 * ALL, UNIT, WX // 2), BF16), vmem((4 * ALL, UNIT, WX // 2), BF16),
        vmem((4 * ALL, UNIT, WX), BF16), vmem((4 * ALL, UNIT, WX), BF16), vmem((4 * ALL, UNIT, WX), BF16),
        vmem((4 * ALL, UNIT, WX // 2), BF16), vmem((4 * ALL, UNIT, WX // 2), BF16),
        vmem((ALL, UNIT, WX), BF16), vmem((ALL, UNIT, WX), BF16),
        vmem((8 * ALL, UNIT, WY), BF16), vmem((8 * ALL, UNIT, WY), BF16),
        vmem((4 * ALL, UNIT, WY), BF16), vmem((4 * ALL, UNIT, WY), BF16),
        vmem((ALL, UNIT, WY // 2), BF16), vmem((ALL, UNIT, WY // 2), BF16),
        vmem((ALL, UNIT, WY), BF16), vmem((ALL, UNIT, WY), BF16), vmem((ALL, UNIT, WY), BF16),
        dma((2 * CHUNKS,)), dma((rows // TILE,)), dma((2 * PIECES,)), of_groups, of_groups, of_pieces, of_pieces, of_groups,
        of_groups, of_groups, of_groups, of_groups, of_groups,
        of_groups, of_pieces, of_pieces, of_groups,
        of_groups, of_pieces, of_pieces, of_groups,
        of_pieces, of_pieces, of_pieces, of_pieces, of_pieces,
    ]
    transposed = pl.pallas_call(
        kernel,
        out_shape=jax.ShapeDtypeStruct((ALL, UNIT, rows), F32),
        in_specs=[pl.BlockSpec(memory_space=pl.ANY)] * 3,
        out_specs=pl.BlockSpec(memory_space=pl.ANY),
        scratch_shapes=scratch,
        compiler_params=pltpu.CompilerParams(
            collective_id=0, has_side_effects=True, vmem_limit_bytes=67043328
        ),
        name="panels",
    )(traces, features, nexts)
    return transposed.reshape(ALL * UNIT, rows).T


def solution(mesh):
    return jax.shard_map(
        shards,
        mesh=mesh,
        in_specs=(P(("col", "depth"), "row"), P(("col", "depth"), "row"), P(("col", "depth"), "row")),
        out_specs=P("row", ("col", "depth")),
        check_vma=False,
    )
```
